32 devices in a mesh: group: 1, expert: 32 (over z, y, x, core), hslice: 1.
Axes of the slice: x: 2, y: 2, z: 4, core: 2. Of those that a mesh axis runs over, the one named last changes fastest.
Arguments:
- tokens: bfloat16 [2048, 3584], P(('group', 'expert')), may hold values from -6 to 6
- routes: int32 [2048, 8], P(('group', 'expert')), may hold values from 0 to 15, all different within a row; in each aligned block of 64 rows (0 to 63, 64 to 127, ...) at most 36 rows name the same one
- gate_values: float32 [2048, 8], P(('group', 'expert')), may hold values from 0.1 to 1
- gate_up: bfloat16 [32, 3584, 2, 512], P('expert', None, None, 'hslice'), may hold values from -0.09375 to 0.09375
- down_weight: bfloat16 [32, 512, 3584], P('expert', None, 'hslice'), may hold values from -0.1875 to 0.1875
Outputs:
- mixed_out: bfloat16 [2048, 3584], P(('group', 'expert'), 'hslice')
The draws below stay inside these ranges and needn't reach their ends.
Inputs may be any that keep to these rules, and one draw needn't show every extreme that they name: `routes`: each row names 8 different experts. Within the rows of one index of expert (aligned blocks of 64 tokens) no expert is named more than 36 times, a bound that some block reaches.
All inputs are finite; a program needn't handle non-finite values.
Results may differ from the reference program's by a relative error of at most 0.0065.
Values may be sent and summed in bfloat16 or wider, within the bound.
No kernel may reach another device: no remote copies, remote signals or barrier semaphores. Data moves between devices by JAX's collectives and lax.ppermute only.
A program may use at most 64 MiB of HBM per device.

```python
import math
import jax
import jax.numpy as jnp
import numpy as np
from jax import lax

D = 3584
FF = 1024
TOK_DEV = 64
EXPERTS = 16
TOPK = 8
CAP = 36
TOKENS = 2048
N_EXPERT = 32


def level_of(rng, extent, pieces, low, high):
    gain, own = 1.0, jax.random.fold_in(rng, 6)
    for dim, shards_of in pieces:
        heights = jnp.exp(jax.random.uniform(jax.random.fold_in(own, dim), (shards_of,), jnp.float32, low / len(pieces), high / len(pieces)))
        gain = gain * jnp.repeat(heights, extent[dim] // shards_of).reshape([-1 if axis == dim else 1 for axis in range(len(extent))])
    return gain


def shared_out(own_key, own, number, rows, amount, top, reach, skew):
    sequence = jax.random.permutation(own_key, amount)
    crowded, common = portions_of(amount, rows * top, reach, skew, True), portions_of(amount, rows * top, reach, skew, False)
    places = jnp.arange(amount)

    def named(sizes, rotation):
        used = int((sizes > 0).sum())
        fixed = max(1, used // 4)
        passed = fixed + (places - fixed + rotation * (used - fixed)) % max(1, amount - fixed)
        return jnp.zeros((amount,), jnp.int32).at[sequence[jnp.where(places < fixed, places, passed)]].set(jnp.asarray(sizes, jnp.int32))

    sizes = jnp.where(number % 4 == 0, named(crowded, number // 4), named(common, number - number // 4 - 1))
    mixed = jax.random.permutation(jax.random.fold_in(own, 3), amount)
    source_of, sink = mixed[0:amount // 2 * 2:2], mixed[1:amount // 2 * 2:2]
    room = jnp.minimum(sizes[source_of] - 1, reach - sizes[sink]) // 2
    room = jnp.where((source_of == sequence[0]) | (sink == sequence[0]) | (sizes[sink] == 0), 0, jnp.maximum(room, 0))
    passed = jax.random.randint(jax.random.fold_in(own, 4), (amount // 2,), 0, 1 << 20) % (room + 1)
    sizes = sizes.at[source_of].add(-passed).at[sink].add(passed)
    members = jnp.searchsorted(jnp.cumsum(sizes), jnp.arange(rows * top), side="right").astype(jnp.int32)
    listing = members.reshape(top, rows).T
    listing = listing[jax.random.permutation(jax.random.fold_in(own, 1), rows)]
    rotation = jax.random.randint(jax.random.fold_in(own, 2), (rows, 1), 0, top)
    return jnp.take_along_axis(listing, (jnp.arange(top)[None, :] + rotation) % top, axis=1)


def portions_of(amount, total, most, skew, full):
    portions = [(1 << 20) // math.isqrt(standing ** skew) + 1 for standing in range(1, amount + 1)]
    largest = most if full else min(most, max(-(-total // amount), total * portions[0] // sum(portions)))
    least = 1 if total - largest >= amount - 1 else 0
    given, surplus = [largest] + [least] * (amount - 1), total - largest - least * (amount - 1)
    while surplus > 0:
        free = [i for i in range(1, amount) if given[i] < largest] or [i for i in range(1, amount) if given[i] < most]
        mass, remaining = sum([portions[i] for i in free]), surplus
        for i in free:
            addition = min(most - given[i], max(1, remaining * portions[i] // mass), surplus)
            given[i] = given[i] + addition
            surplus = surplus - addition
    return np.array(given)


def bell_draw(key, dims, width, reach, split=(), kind=jnp.bfloat16):
    loudness = level_of(key, dims, split, -0.22, 0.18) if split else 1.0
    result = jax.random.normal(key, dims, jnp.float32) * width * loudness
    return jnp.minimum(jnp.maximum(result, -reach), reach).astype(kind)


def setup_inputs(seed: int = 0, part: int = 0) -> dict:
    key_of = jax.random.split(jax.random.key(seed), 6)
    part_keys = jax.random.split(jax.random.fold_in(key_of[5], part), 6)
    tokens = bell_draw(part_keys[0], (TOKENS, D), 1.0, 6.0, ((0, 32),))
    routes_keys = jax.random.split(jax.random.fold_in(part_keys[1], 1), TOKENS // TOK_DEV)
    routes_turns = jax.random.permutation(jax.random.fold_in(part_keys[1], 3), TOKENS // TOK_DEV)
    routes = jax.vmap(lambda own, number: shared_out(jax.random.fold_in(part_keys[1], 2), own, number, TOK_DEV, EXPERTS, TOPK, CAP, 2))(routes_keys, routes_turns).reshape((TOKENS, TOPK))
    gate_values = jnp.clip(0.1 + 0.9 * jax.random.uniform(part_keys[2], (TOKENS, TOPK), jnp.float32) ** level_of(part_keys[2], (TOKENS, TOPK), ((0, 32),), -0.2, 0.2), 0.1, 1.0)
    gate_up = bell_draw(key_of[3], (2 * EXPERTS, D, 2, FF // 2), D ** -0.5, 0.09375, ((0, 32),))
    down_weight = bell_draw(key_of[4], (2 * EXPERTS, FF // 2, D), FF ** -0.5, 0.1875, ((0, 32),))
    return {"tokens": tokens, "routes": routes, "gate_values": gate_values, "gate_up": gate_up, "down_weight": down_weight}


def reference(tokens, routes, gate_values, gate_up, down_weight):
    expert_ids = routes.reshape(-1).astype(jnp.int32)
    member = (expert_ids[:, None] == jnp.arange(EXPERTS, dtype=jnp.int32)[None, :]).astype(jnp.int32)
    blocks = member.reshape(N_EXPERT, TOK_DEV * TOPK, EXPERTS)
    before = (jnp.cumsum(blocks, axis=1) - blocks).astype(jnp.int32)
    position = jnp.sum(before * blocks, axis=2).astype(jnp.int32).reshape(-1)
    source = jnp.arange(TOKENS * TOPK, dtype=jnp.int32) // (TOK_DEV * TOPK)
    token_row = jnp.arange(TOKENS * TOPK, dtype=jnp.int32) // TOPK
    slot_table = jnp.zeros((EXPERTS, N_EXPERT, CAP), jnp.int32).at[expert_ids, source, position].set(token_row)
    half_units = FF // 2

    def one_expert(expert_index):
        inputs = jnp.take(tokens, slot_table[expert_index].reshape(-1), axis=0)
        weight_pair = lax.dynamic_slice_in_dim(gate_up, 2 * expert_index, 2, 0)
        gate_matrix = jnp.transpose(weight_pair[:, :, 0, :], (1, 0, 2)).reshape(D, FF)
        up_matrix = jnp.transpose(weight_pair[:, :, 1, :], (1, 0, 2)).reshape(D, FF)
        down_matrix = lax.dynamic_slice_in_dim(down_weight, 2 * expert_index, 2, 0).reshape(FF, D)
        gate_value = jnp.dot(inputs, gate_matrix, preferred_element_type=jnp.float32)
        up_value = jnp.dot(inputs, up_matrix, preferred_element_type=jnp.float32)
        hidden = (jax.nn.silu(gate_value) * up_value).astype(jnp.bfloat16)
        summed = jnp.zeros((N_EXPERT * CAP, D), jnp.float32)
        for segment in range(2):
            offset = segment * half_units
            partial_value = jnp.dot(hidden[:, offset:offset + half_units], down_matrix[offset:offset + half_units], preferred_element_type=jnp.float32)
            partial_value = lax.optimization_barrier(partial_value.astype(jnp.bfloat16))
            summed = summed + partial_value.astype(jnp.float32)
        return lax.optimization_barrier(summed.astype(jnp.bfloat16))

    outputs = lax.map(one_expert, jnp.arange(EXPERTS, dtype=jnp.int32))
    flat_index = ((expert_ids * N_EXPERT + source) * CAP + position).astype(jnp.int32)
    picked = jnp.take(outputs.reshape(EXPERTS * N_EXPERT * CAP, D), flat_index, axis=0).astype(jnp.float32)
    mixed_out = jnp.sum(picked.reshape(TOKENS, TOPK, D) * gate_values[:, :, None], axis=1)
    return mixed_out.astype(jnp.bfloat16)
```

```python
import functools

import jax
import jax.numpy as jnp
from jax import lax
from jax.experimental import pallas as pl
from jax.experimental.pallas import tpu as pltpu
from jax.sharding import PartitionSpec as P


BF16 = jnp.bfloat16
F32 = jnp.float32
NO_SLOT = -1024.0
VMEM_LIMIT = 24 * 1024 * 1024


def swap(block, mask, count):
    route = [(i, i ^ mask) for i in range(count)]
    return lax.ppermute(block, "expert", route)


def call(body, outs, args, scratch=(), flops=0, name=None):
    nbytes = sum(a.size * a.dtype.itemsize for a in args)
    nbytes += sum(o.size * o.dtype.itemsize for o in outs)
    specs = [
        pl.BlockSpec(memory_space=pltpu.SMEM if a.ndim == 1 else pltpu.VMEM) for a in args
    ]
    return pl.pallas_call(
        body,
        out_shape=outs,
        in_specs=specs,
        out_specs=[pl.BlockSpec(memory_space=pltpu.VMEM)] * len(outs),
        scratch_shapes=list(scratch),
        compiler_params=pltpu.CompilerParams(vmem_limit_bytes=VMEM_LIMIT),
        cost_estimate=pl.CostEstimate(flops=flops, bytes_accessed=nbytes, transcendentals=0),
        name=name,
    )(*args)


def shape(*dims):
    return jax.ShapeDtypeStruct(dims, BF16)


def prepare_body(experts, cap, meta, core, tokens, routes, gates, own, send):
    rows, features = tokens.shape
    half = features // 2
    choices = routes.shape[1]
    me = core[0]
    lane = lax.broadcasted_iota(jnp.int32, (rows, meta), 1)
    member = jnp.zeros((rows, meta), F32)
    parts = jnp.zeros((rows, meta), F32)
    for k in range(choices):
        route = routes[:, k : k + 1]
        gate = gates[:, k : k + 1]
        high = gate.astype(BF16).astype(F32)
        rest = gate - high
        middle = rest.astype(BF16).astype(F32)
        low = rest - middle
        member += jnp.where(lane == route, 1.0, 0.0)
        for j, part in enumerate((high, middle, low)):
            parts += jnp.where(lane == route + (j + 1) * experts, part, 0.0)
    row_id = lax.broadcasted_iota(jnp.int32, (rows, rows), 0)
    col_id = lax.broadcasted_iota(jnp.int32, (rows, rows), 1)
    earlier = jnp.where(col_id < row_id, 1.0, 0.0).astype(BF16)
    position = jnp.dot(earlier, member.astype(BF16), preferred_element_type=F32)
    slot = jnp.where(member > 0.5, position + (me * cap).astype(F32), NO_SLOT)
    table = jnp.where(lane < experts, slot, parts).astype(BF16)
    own[:, half:] = table
    send[:, half:] = table
    mine = pl.multiple_of(me * half, 128)
    other = pl.multiple_of((1 - me) * half, 128)
    own[:, :half] = tokens[:, pl.ds(mine, half)]
    send[:, :half] = tokens[:, pl.ds(other, half)]


def column(table, index):
    lane = lax.broadcasted_iota(jnp.int32, table.shape, 1)
    return jnp.sum(jnp.where(lane == index, table, 0.0), axis=1, keepdims=True)


def select_body(slots, near, ids, block, *outs):
    rows = block.shape[0]
    half = outs[0].shape[1]
    table = block[:, half:].astype(F32)
    lane = lax.broadcasted_iota(jnp.int32, (rows, near * slots), 1).astype(F32)
    hot = jnp.zeros((rows, near * slots), F32)
    for j in range(near):
        hot += jnp.where(column(table, ids[j]) + float(j * slots) == lane, 1.0, 0.0)
    hot = hot.astype(BF16)
    picked = lax.dot_general(
        hot, block[:, :half], (((0,), (0,)), ((), ())), preferred_element_type=F32
    ).astype(BF16)
    for j in range(near):
        outs[j][...] = picked[j * slots : (j + 1) * slots]


def gate_up_body(near, core, *refs):
    mine, theirs = refs[:near], refs[near : 2 * near]
    weights, hidden = refs[2 * near], refs[2 * near + 1]
    half = mine[0].shape[1]
    width = weights.shape[1] // 2
    me = core[0]
    own_at = pl.multiple_of(me * half, 128)
    other_at = pl.multiple_of((1 - me) * half, 128)
    left = jnp.concatenate([r[...] for r in mine], axis=0)
    right = jnp.concatenate([r[...] for r in theirs], axis=0)
    tile = min(width, 256)
    for at in range(0, width, tile):
        both = []
        for base in (0, width):
            cols = slice(base + at, base + at + tile)
            total = jnp.dot(left, weights[pl.ds(own_at, half), cols], preferred_element_type=F32)
            total += jnp.dot(
                right, weights[pl.ds(other_at, half), cols], preferred_element_type=F32
            )
            both.append(total)
        gate, up = both
        hidden[:, at : at + tile] = (gate / (1.0 + jnp.exp(-gate)) * up).astype(BF16)


def down_body(core, hidden, weights, keep, send):
    half = keep.shape[1]
    me = core[0]
    tile = 256 if half % 256 == 0 else 128
    for at in range(0, half, tile):
        for out, which in ((keep, me), (send, 1 - me)):
            cols = pl.ds(pl.multiple_of(which * half + at, 128), tile)
            out[:, at : at + tile] = jnp.dot(
                hidden[...], weights[:, cols], preferred_element_type=F32
            ).astype(BF16)


def pair_body(near, keep, received, *outs):
    slots = keep.shape[0] // near
    total = (keep[...].astype(F32) + received[...].astype(F32)).astype(BF16)
    for j in range(near):
        outs[j][...] = total[j * slots : (j + 1) * slots]


def weighted(experts, near, ids, block, half_in, rows):
    count = block.shape[0]
    slots = rows[0].shape[0]
    table = block[:, half_in:].astype(F32)
    lane = lax.broadcasted_iota(jnp.int32, (count, slots), 1).astype(F32)
    total = None
    for j in range(near):
        at = column(table, ids[j]) == lane
        stack = [
            jnp.where(at, column(table, ids[j] + (p + 1) * experts), 0.0).astype(BF16)
            for p in range(3)
        ]
        part = jnp.dot(
            jnp.concatenate(stack, axis=0), rows[j][...], preferred_element_type=F32
        )
        part = part[:count] + part[count : 2 * count] + part[2 * count :]
        total = part if total is None else total + part
    return total


def combine_body(experts, near, half_in, ids, block, *refs):
    rows, out = refs[:near], refs[near]
    out[...] = weighted(experts, near, ids, block, half_in, rows).astype(BF16)


def finish_body(experts, near, half_in, ids, block, *refs):
    rows, sums, outs = refs[:near], refs[near:-2], refs[-2:]
    total = weighted(experts, near, ids, block, half_in, rows)
    for other in sums:
        total += other[...].astype(F32)
    count = total.shape[0] // 2
    total = total.astype(BF16)
    outs[0][...] = total[:count]
    outs[1][...] = total[count:]


def join_body(core, own, received, out):
    half = own.shape[1]
    me = core[0]
    out[:, pl.ds(pl.multiple_of(me * half, 128), half)] = own[...]
    out[:, pl.ds(pl.multiple_of((1 - me) * half, 128), half)] = received[...]


def local(tokens, routes, gate_values, gate_up, down_weight):
    devices = lax.axis_size("expert")
    experts = devices // 2
    near = 1
    while 4 * near * near <= experts:
        near *= 2
    far = experts // near
    tok_count, choices = routes.shape
    features = tokens.shape[1]
    half_in = features // 2
    hidden_width = gate_up.shape[3]
    half_units = down_weight.shape[1]
    columns = down_weight.shape[2]
    capacity = min(tok_count, 2 * ((9 * tok_count * choices + 16 * experts - 1) // (16 * experts)))
    slots = 2 * capacity
    meta = -(-4 * experts // 128) * 128

    index = lax.axis_index("expert").astype(jnp.int32)
    core = (index % 2).reshape(1)
    chip = index // 2
    ids = (chip // near) * near + jnp.bitwise_xor(chip % near, jnp.arange(near, dtype=jnp.int32))

    own, send = call(
        functools.partial(prepare_body, experts, capacity, meta),
        [shape(tok_count, half_in + meta)] * 2,
        [core, tokens, routes, gate_values],
        name="prepare",
    )
    received = swap(send, 1, devices)
    block = jnp.concatenate([own, received], axis=0)
    blocks = [block] + [swap(block, 2 * near * k, devices) for k in range(1, far)]

    weights = gate_up.reshape(features, 2 * hidden_width)
    down = down_weight.reshape(half_units, columns)
    padded = -(-columns // 256) * 256
    if padded != columns:
        down = jnp.pad(down, ((0, 0), (0, padded - columns)))
    half_out = padded // 2

    def to_experts(source):
        picked = call(
            functools.partial(select_body, slots, near),
            [shape(slots, half_in)] * near,
            [ids, source],
            name="select",
        )
        return [picked[0]] + [swap(picked[j], 2 * j, devices) for j in range(1, near)]

    def expert(mine):
        theirs = [swap(part, 1, devices) for part in mine]
        rows = near * slots
        (hidden,) = call(
            functools.partial(gate_up_body, near),
            [shape(rows, hidden_width)],
            [core] + list(mine) + theirs + [weights],
            flops=4 * rows * features * hidden_width,
            name="gate_up",
        )
        hidden = lax.all_gather(hidden, "hslice", axis=1, tiled=True)
        keep, send = call(
            down_body,
            [shape(rows, half_out)] * 2,
            [core, hidden, down],
            flops=2 * rows * half_units * padded,
            name="down",
        )
        return keep, swap(send, 1, devices)

    def to_tokens(keep, received):
        totals = call(
            functools.partial(pair_body, near),
            [shape(slots, half_out)] * near,
            [keep, received],
            name="pair",
        )
        return [totals[0]] + [swap(totals[j], 2 * j, devices) for j in range(1, near)]

    mine = [to_experts(source) for source in blocks]
    results = [expert(part) for part in mine]
    rows = [None] * far
    for k in list(range(far - 1, -1, -1)):
        rows[k] = to_tokens(*results[k])
    sums = []
    for k in range(far - 1, 0, -1):
        (partial,) = call(
            functools.partial(combine_body, experts, near, half_in),
            [shape(2 * tok_count, half_out)],
            [ids, blocks[k]] + rows[k],
            name="combine",
        )
        sums.append(swap(partial, 2 * near * k, devices))
    own, send = call(
        functools.partial(finish_body, experts, near, half_in),
        [shape(tok_count, half_out)] * 2,
        [ids, blocks[0]] + rows[0] + sums,
        name="finish",
    )
    received = swap(send, 1, devices)
    (out,) = call(join_body, [shape(tok_count, padded)], [core, own, received], name="join")
    return out[:, :columns]


def solution(mesh):
    in_specs = (
        P(("group", "expert"), None),
        P(("group", "expert"), None),
        P(("group", "expert"), None),
        P("expert", None, None, "hslice"),
        P("expert", None, "hslice"),
    )
    out_specs = P(("group", "expert"), "hslice")
    return jax.shard_map(local, mesh=mesh, in_specs=in_specs, out_specs=out_specs, check_vma=False)
```
